256 devices in a mesh: occa: 8 (over x, core), occb: 4 (over z_lo), rows: 8 (over z_hi, y).
Axes of the slice: x: 4, y: 4, z: 8 (z_hi: 2, z_lo: 4; z = z_hi * 4 + z_lo), core: 2. Of those that a mesh axis runs over, the one named last changes fastest.
Arguments:
- density: float32 [512, 8, 4, 2, 512], P('rows', 'occa', 'occb'), may hold values from -6 to 6
- operators: float32 [5, 512, 512], P(None, 'rows'), as said below
- rates: float32 [2], replicated, may hold values from 0.05 to 0.5
- coupling: float32 [2, 2], replicated, may hold values from 0.3 to 1
- keep_mask: int32 [8, 4], P('occa', 'occb'), may hold values 0 or 1
Outputs:
- advanced: float32 [512, 8, 4, 2, 512], P('rows', 'occa', 'occb')
The draws below stay inside these ranges and needn't reach their ends.
Inputs may be any that keep to these rules, and one draw needn't show every extreme that they name: `keep_mask`: 1 keeps an auxiliary matrix in the hierarchy, 0 removes it. `operators`: each of the five matrices is symmetric.
All inputs are finite; a program needn't handle non-finite values. No bound on the sum of `keep_mask` on one device may be relied on, other than what follows from the above.
Results may differ from the reference program's by a relative error of at most 0.00005.
Values sent between devices are 32-bit elements; how exact they have to be, the bound alone decides.
A program may use at most 64 MiB of HBM per device.

```python
import math
import jax
import jax.numpy as jnp
from jax import lax

M = 512
NA = 8
NB = 4


def draw_operators(key, part):
    sampled = jax.random.normal(key, (5, M, M), jnp.float32)
    return (sampled + jnp.swapaxes(sampled, 1, 2)) / jnp.sqrt(2.0 * M)


def place_ends(values, own_key, low, high):
    extent = values.shape
    place = [jax.random.randint(jax.random.fold_in(own_key, axis), (), 0, extent[axis]) for axis in range(len(extent))]
    values = values.at[tuple(place)].set(low)
    longest = extent.index(max(extent))
    place[longest] = (place[longest] + 1) % extent[longest]
    return values.at[tuple(place)].set(high)


def levels(key, extent, shards, smallest, high):
    gain, own = 1.0, jax.random.fold_in(key, 6)
    for dim, parts in shards:
        steps = jnp.exp(jax.random.uniform(jax.random.fold_in(own, dim), (parts,), jnp.float32, smallest / len(shards), high / len(shards)))
        gain = gain * jnp.repeat(steps, extent[dim] // parts).reshape([-1 if axis == dim else 1 for axis in range(len(extent))])
    return gain


def normal_values(rng, dims, scale, reach, pieces=(), held_as=jnp.bfloat16):
    loudness = levels(rng, dims, pieces, -0.22, 0.18) if pieces else 1.0
    array = jax.random.normal(rng, dims, jnp.float32) * scale * loudness
    return jnp.minimum(jnp.maximum(array, -reach), reach).astype(held_as)


def setup_inputs(seed: int = 0) -> dict:
    seeds = jax.random.split(jax.random.key(seed), 6)
    density = normal_values(seeds[0], (M, NA, NB, 2, M), 1.0, 6.0, ((0, 8), (1, 8), (2, 4)), jnp.float32)
    operators = draw_operators(jax.random.fold_in(seeds[5], 71), 0)
    rates = jnp.clip(jnp.exp(jax.random.uniform(seeds[2], (2,), jnp.float32, math.log(0.05), math.log(0.5))), 0.05, 0.5)
    coupling = jnp.clip(jax.random.uniform(seeds[3], (2, 2), jnp.float32, 0.3, 1.0), 0.3, 1.0)
    keep_mask = place_ends((jax.random.randint(seeds[4], (NA, NB), 0, 4) < 3).astype(jnp.int32), jax.random.fold_in(seeds[4], 1), 0, 1)
    return {"density": density, "operators": operators, "rates": rates, "coupling": coupling, "keep_mask": keep_mask}


TIME_STEP = 0.05
PRECISE = lax.Precision.HIGHEST

def neighbours(extended, count_a, count_b):
    return jnp.stack([extended[:, 1:count_a + 1, 1:count_b + 1], extended[:, 2:count_a + 2, 1:count_b + 1], extended[:, 0:count_a, 1:count_b + 1], extended[:, 1:count_a + 1, 2:count_b + 2], extended[:, 1:count_a + 1, 0:count_b]], axis=3)

def ladder_factors(occ_a, occ_b, coupling):
    zeros = jnp.zeros_like(occ_a + occ_b)
    up_a = jnp.sqrt(occ_a + 1.0) + zeros
    up_b = jnp.sqrt(occ_b + 1.0) + zeros
    down_a = jnp.sqrt(occ_a) + zeros
    down_b = jnp.sqrt(occ_b) + zeros
    factor_re = jnp.stack([zeros, zeros, down_a * coupling[0, 1], zeros, down_b * coupling[1, 1]], axis=-1)
    factor_im = jnp.stack([zeros - 1.0, -up_a, -down_a * coupling[0, 0], -up_b, -down_b * coupling[1, 0]], axis=-1)
    return (factor_re, factor_im)

def weighted(stacked, factor_re, factor_im):
    part_re = stacked[..., 0, :]
    part_im = stacked[..., 1, :]
    scale_re = factor_re[None, :, :, :, None]
    scale_im = factor_im[None, :, :, :, None]
    return jnp.stack([scale_re * part_re - scale_im * part_im, scale_re * part_im + scale_im * part_re], axis=4)

def derivative(field, operators, factor_re, factor_im, damping, kept):
    extended = jnp.pad(field, ((0, 0), (1, 1), (1, 1), (0, 0), (0, 0)))
    stacked = neighbours(extended, NA, NB)
    left_ops = weighted(stacked, factor_re, factor_im)
    right_ops = weighted(stacked, factor_re, -factor_im)
    left_part = jnp.einsum('kic,cabkpm->iabpm', operators, left_ops, precision=PRECISE)
    right_part = jnp.einsum('iabkpc,kcm->iabpm', right_ops, operators, precision=PRECISE)
    return (left_part + right_part - damping * field) * kept

def reference(density, operators, rates, coupling, keep_mask):
    occ_a = jnp.arange(NA).astype(jnp.float32)[:, None]
    occ_b = jnp.arange(NB).astype(jnp.float32)[None, :]
    factor_re, factor_im = ladder_factors(occ_a, occ_b, coupling)
    damping = (occ_a * rates[0] + occ_b * rates[1])[None, :, :, None, None]
    kept = keep_mask.astype(jnp.float32)[None, :, :, None, None]
    start = density * kept
    first = derivative(start, operators, factor_re, factor_im, damping, kept)
    second = derivative(first, operators, factor_re, factor_im, damping, kept)
    return start + TIME_STEP * first + 0.5 * TIME_STEP * TIME_STEP * second
```

```python
import jax
import jax.numpy as jnp
from jax import lax
from jax.experimental import pallas as pl
from jax.experimental.pallas import tpu as pltpu
from jax.sharding import PartitionSpec as P

TIME_STEP = 0.05
MESH = pl.DeviceIdType.MESH
F32 = jnp.float32
BF16 = jnp.bfloat16
SITES = 512
OPS = 5
ROWS = 64
COLS = 16
PLANE = 32
COUNT_A = 8
COUNT_B = 4
OWN = COUNT_B


def split(value):
    high = value.astype(BF16)
    low = (value - high.astype(F32)).astype(BF16)
    return high, low


def kernel(
    par, dens, ops, keep, out,
    own, oth, whi, wlo, ghl,
    sent_r, cols_buf, held_c, pack, first_r, first_c,
    near_r, near_c, keeps,
    a_send, a_recv, n_send, n_recv, k_send, k_recv, o_send, o_recv,
):
    ia = lax.axis_index("occa")
    ib = lax.axis_index("occb")
    ir = lax.axis_index("rows")
    half = ir // 4
    iy = lax.rem(ir, 4)
    ix = ia // 2
    core = lax.rem(ia, 2)
    iz = half * 4 + ib
    me_col = iz * 4 + iy
    me_row = ib * 8 + ir

    def a_dev(step):
        return {"occa": lax.rem(ia + step + COUNT_A, COUNT_A)}

    def z_dev(step):
        z = lax.rem(iz + step + 8, 8)
        return {"occb": lax.rem(z, 4), "rows": (z // 4) * 4 + iy}

    def y_dev(step):
        return {"rows": half * 4 + lax.rem(iy + step, 4)}

    def partner(j):
        z = lax.rem(iz + j // 4, 8)
        y = lax.rem(iy + lax.rem(j, 4), 4)
        b = lax.rem(z, 4)
        r = (z // 4) * 4 + y
        return {"occb": b, "rows": r}, z * 4 + y, b * 8 + r

    sibling = {"occa": ix * 2 + 1 - core}

    def remote(src, dst, send, recv, dev):
        return pltpu.make_async_remote_copy(
            src_ref=src, dst_ref=dst, send_sem=send, recv_sem=recv, device_id=dev, device_id_type=MESH
        )

    def block(index):
        return pl.ds(pl.multiple_of(index * COLS, COLS), COLS)

    def to_columns(slot, j):
        dev, col, row = partner(j)
        return remote(sent_r.at[slot, block(col)], cols_buf.at[slot, block(me_row)],
                      a_send.at[slot, j], a_recv.at[slot, me_row], dev)

    def to_rows(slot, j):
        dev, col, row = partner(j)
        return remote(pack.at[slot - 2, block(row)], cols_buf.at[slot, block(me_col)],
                      a_send.at[slot, j], a_recv.at[slot, me_col], dev)

    def start_columns(slot):
        def body(j, carry):
            to_columns(slot, j).start()
            return carry
        lax.fori_loop(1, PLANE, body, 0)
        cols_buf[slot, block(me_row), :] = sent_r[slot, block(me_col), :]

    def start_rows(slot):
        def body(j, carry):
            to_rows(slot, j).start()
            return carry
        lax.fori_loop(1, PLANE, body, 0)
        cols_buf[slot, block(me_col), :] = pack[slot - 2, block(me_row), :]

    def finish_recv(slot, by_row):
        def body(j, carry):
            dev, col, row = partner(j)
            index = row if by_row else col
            piece = cols_buf.at[slot, block(index)]
            remote(piece, piece, a_send.at[slot, j], a_recv.at[slot, index], dev).wait_recv()
            return carry
        lax.fori_loop(1, PLANE, body, 0)

    def finish_send(slot):
        def body(j, carry):
            (to_columns if slot < 2 else to_rows)(slot, j).wait_send()
            return carry
        lax.fori_loop(1, PLANE, body, 0)

    lanes = lax.broadcasted_iota(jnp.int32, (COLS, 128), 1) < 64

    def unpack(slot):
        parts = []
        for b in range(COUNT_B):
            real, imag = [], []
            for t in range(4):
                q = (b * 8 + 2 * t) * COLS
                even = cols_buf[slot, q:q + COLS, :]
                odd = cols_buf[slot, q + COLS:q + 2 * COLS, :]
                real.append(jnp.where(lanes, even, pltpu.roll(odd, 64, 1)))
                imag.append(jnp.where(lanes, pltpu.roll(even, 64, 1), odd))
            parts.append(jnp.concatenate(real, axis=1))
            parts.append(jnp.concatenate(imag, axis=1))
        return jnp.concatenate(parts, axis=0)

    def repack(slot, value):
        for b in range(COUNT_B):
            for t in range(4):
                real = value[32 * b:32 * b + COLS, 128 * t:128 * t + 128]
                imag = value[32 * b + COLS:32 * b + 32, 128 * t:128 * t + 128]
                q = (b * 8 + 2 * t) * COLS
                pack[slot - 2, q:q + COLS, :] = jnp.where(lanes, real, pltpu.roll(imag, 64, 1))
                pack[slot - 2, q + COLS:q + 2 * COLS, :] = jnp.where(lanes, pltpu.roll(real, 64, 1), imag)

    def put(k, row, value):
        high, low = split(value)
        count = value.shape[0]
        ghl[row:row + count, k * SITES:(k + 1) * SITES] = high
        ghl[128 + row:128 + row + count, k * SITES:(k + 1) * SITES] = low

    def multiply():
        both = jnp.dot(ghl[...], whi[...], preferred_element_type=F32)
        rest = jnp.dot(ghl[0:128, :], wlo[...], preferred_element_type=F32)
        return both[0:128] + both[128:256] + rest

    def right(center, base):
        fields = [center, near_r.at[base], near_r.at[base + 1], near_r.at[base + 2], near_r.at[base + 3]]
        for k, field in enumerate(fields):
            re, im = field[0:ROWS, :], field[ROWS:128, :]
            f_re, f_im = par[OWN, 2 * k], par[OWN, 2 * k + 1]
            put(k, 0, f_re * re + f_im * im)
            put(k, ROWS, f_re * im - f_im * re)
        return multiply()

    def left(center, base):
        for b in range(COUNT_B):
            for k in range(OPS):
                source, at = center, b
                if k == 1:
                    source = near_c.at[base]
                elif k == 2:
                    source = near_c.at[base + 1]
                elif k == 3:
                    at = min(b + 1, COUNT_B - 1)
                elif k == 4:
                    at = max(b - 1, 0)
                re = source[32 * at:32 * at + COLS, :]
                im = source[32 * at + COLS:32 * at + 32, :]
                f_re, f_im = par[b, 2 * k], par[b, 2 * k + 1]
                put(k, 32 * b, f_re * re - f_im * im)
                put(k, 32 * b + COLS, f_re * im + f_im * re)
        return multiply()

    def near_copy(kind, index, src, dst, dev):
        return remote(src, dst, n_send.at[kind, index], n_recv.at[kind, index], dev)

    def row_moves(kind, src):
        base = 4 * kind
        return [
            near_copy(kind, 0, src, near_r.at[base], a_dev(-1)),
            near_copy(kind, 1, src, near_r.at[base + 1], a_dev(1)),
            near_copy(kind, 2, src, near_r.at[base + 2], z_dev(-1)),
            near_copy(kind, 3, src, near_r.at[base + 3], z_dev(1)),
        ]

    def col_moves(kind, src):
        base = 2 * kind
        return [
            near_copy(2 + kind, 0, src, near_c.at[base], a_dev(-1)),
            near_copy(2 + kind, 1, src, near_c.at[base + 1], a_dev(1)),
        ]

    def eight(index):
        return pl.ds(pl.multiple_of(index * 8, 8), 8)

    def thirty_two(index):
        return pl.ds(pl.multiple_of(index * 32, 32), 32)

    def wide(index):
        return pl.ds(pl.multiple_of(index * 256, 256), 256)

    share = core * 4 + ix
    half_z = remote(ops.at[:, eight(share), wide(half)], oth.at[iy, :, eight(share), :],
                    o_send.at[0], o_recv.at[0], z_dev(4))
    half_y = [remote(oth.at[iy, :, eight(share), :], oth.at[iy, :, eight(share), :],
                     o_send.at[s], o_recv.at[s], y_dev(s)) for s in (1, 2, 3)]
    half_x = [remote(oth.at[:, :, eight(share), :], oth.at[:, :, eight(share), :],
                     o_send.at[3 + s], o_recv.at[3 + s], a_dev(2 * s)) for s in (1, 2, 3)]
    half_c = remote(oth.at[:, :, thirty_two(core), :], oth.at[:, :, thirty_two(core), :],
                    o_send.at[7], o_recv.at[7], sibling)
    own_y = [remote(ops.at[:, thirty_two(core), :], own.at[iy, :, thirty_two(core), :],
                    o_send.at[7 + s], o_recv.at[7 + s], y_dev(s)) for s in (1, 2, 3)]

    def own_c(s):
        y = lax.rem(iy + 4 - s, 4)
        return remote(own.at[y, :, thirty_two(core), :], own.at[y, :, thirty_two(core), :],
                      o_send.at[10 + s], o_recv.at[10 + s], sibling)

    keep_moves = [remote(keep, keeps.at[ib], k_send.at[s], k_recv.at[s],
                         {"occb": lax.rem(ib + s, COUNT_B)}) for s in (1, 2, 3)]

    barrier = pltpu.get_barrier_semaphore()

    def greet(j, carry):
        dev, col, row = partner(j)
        pl.semaphore_signal(barrier, inc=1, device_id=dev, device_id_type=MESH)
        return carry

    lax.fori_loop(1, PLANE, greet, 0)
    for step in (1, -1, 2, -2, 4):
        pl.semaphore_signal(barrier, inc=1, device_id=a_dev(step), device_id_type=MESH)
    sent_r[0] = dens[...].T
    pl.semaphore_wait(barrier, PLANE - 1 + 5)

    half_z.start()
    start_columns(0)
    for copy in keep_moves:
        copy.start()
    for copy in own_y:
        copy.start()
    start_moves = row_moves(0, dens)
    for copy in start_moves:
        copy.start()
    keeps[ib] = keep[...]

    def put_operator(y, own_rows, other_rows):
        base = half * 256 + y * ROWS
        for k in range(OPS):
            at = pl.ds(pl.multiple_of(k * SITES + base, ROWS), ROWS)
            high, low = split(own_rows[k])
            whi[at, :] = high
            wlo[at, :] = low

    half_z.wait_recv()
    for copy in half_y:
        copy.start()

    put_operator(iy, ops, None)

    for copy in half_y:
        copy.wait_recv()
    for copy in half_y:
        copy.wait_send()
    half_x_started = half_x
    for copy in half_x_started:
        copy.start()

    finish_recv(0, True)
    held_c[...] = unpack(0)
    start_cols = col_moves(0, held_c)
    for copy in start_cols:
        copy.start()

    own_moves = []
    for s in (1, 2, 3):
        own_y[s - 1].wait_recv()
        copy = own_c(s)
        copy.start()
        own_moves.append(copy)
    for copy in half_x:
        copy.wait_recv()
    for copy in half_x:
        copy.wait_send()
    half_c.start()

    for s in (1, 2, 3):
        y = lax.rem(iy + 4 - s, 4)
        own_moves[s - 1].wait_recv()
        put_operator(y, own.at[y], None)

    for k in range(OPS):
        source = pl.ds(pl.multiple_of(k * SITES + half * 256, 256), 256)
        target = pl.ds(pl.multiple_of(k * SITES + (1 - half) * 256, 256), 256)
        whi[target, wide(half)] = whi[source, wide(1 - half)].T
        wlo[target, wide(half)] = wlo[source, wide(1 - half)].T
    half_c.wait_recv()
    for k in range(OPS):
        for y in range(4):
            at = pl.ds(pl.multiple_of(k * SITES + (1 - half) * 256 + y * ROWS, ROWS), ROWS)
            high, low = split(oth[y, k])
            whi[at, wide(1 - half)] = high
            wlo[at, wide(1 - half)] = low

    for copy in start_moves:
        copy.wait_recv()
    kept = par[OWN, 11]
    damp = par[OWN, 10]
    first_r[...] = kept * (right(dens, 0) - damp * dens[...])
    sent_r[1] = first_r[...].T
    start_columns(1)

    for copy in start_cols:
        copy.wait_recv()
    for copy in keep_moves:
        copy.wait_recv()
    kept_c = jnp.concatenate(
        [jnp.broadcast_to(keeps[b, 0:1, 0:1], (2 * COLS, SITES)) for b in range(COUNT_B)], axis=0
    )
    first_c[...] = kept_c * left(held_c, 0)
    repack(2, first_c[...])
    start_rows(2)

    finish_recv(1, True)
    first_c[...] += unpack(1)
    next_cols = col_moves(1, first_c)
    for copy in next_cols:
        copy.start()
    finish_recv(2, False)
    first_r[...] += cols_buf[2].T
    next_moves = row_moves(1, first_r)
    for copy in next_moves:
        copy.start()

    for copy in next_cols:
        copy.wait_recv()
    repack(3, left(first_c, 2))
    start_rows(3)

    for copy in next_moves:
        copy.wait_recv()
    second = right(first_r, 4) - damp * first_r[...]
    finish_recv(3, False)
    second = kept * (second + cols_buf[3].T)
    out[...] = dens[...] + TIME_STEP * first_r[...] + (0.5 * TIME_STEP * TIME_STEP) * second

    half_z.wait_send()
    for slot in range(4):
        finish_send(slot)
    half_c.wait_send()
    for copy in keep_moves + own_y + own_moves + start_moves + start_cols + next_cols + next_moves:
        copy.wait_send()


def parameters(rates, coupling, keep_mask):
    occ_a = lax.axis_index("occa").astype(F32)
    own_b = lax.axis_index("occb")
    index_b = jnp.concatenate([jnp.arange(COUNT_B), own_b[None]])
    occ_b = index_b.astype(F32)
    ones = jnp.ones_like(occ_b)
    zeros = jnp.zeros_like(occ_b)
    up_a = jnp.where(occ_a < COUNT_A - 1, jnp.sqrt(occ_a + 1.0), 0.0) * ones
    up_b = jnp.where(occ_b < COUNT_B - 1, jnp.sqrt(occ_b + 1.0), 0.0)
    down_a = jnp.sqrt(occ_a) * ones
    down_b = jnp.sqrt(occ_b)
    damping = occ_a * rates[0] + occ_b * rates[1]
    kept = keep_mask[0, 0].astype(F32) * ones
    return jnp.stack(
        [
            zeros, -ones,
            zeros, -up_a,
            down_a * coupling[0, 1], -down_a * coupling[0, 0],
            zeros, -up_b,
            down_b * coupling[1, 1], -down_b * coupling[1, 0],
            damping, kept,
        ],
        axis=1,
    )


def shards(density, operators, rates, coupling, keep_mask):
    kept = keep_mask[0, 0].astype(F32)
    start = (density[:, 0, 0] * kept).transpose(1, 0, 2).reshape(2 * ROWS, SITES)
    keep = jnp.full((8, 128), kept, F32)
    par = parameters(rates, coupling, keep_mask)
    vmem = pl.BlockSpec(memory_space=pltpu.VMEM)
    dma = pltpu.SemaphoreType.DMA
    result = pl.pallas_call(
        kernel,
        out_shape=jax.ShapeDtypeStruct((2 * ROWS, SITES), F32),
        in_specs=[pl.BlockSpec(memory_space=pltpu.SMEM), vmem, vmem, vmem],
        out_specs=vmem,
        scratch_shapes=[
            pltpu.VMEM((4, OPS, ROWS, SITES), F32),
            pltpu.VMEM((4, OPS, ROWS, SITES // 2), F32),
            pltpu.VMEM((OPS * SITES, SITES), BF16),
            pltpu.VMEM((OPS * SITES, SITES), BF16),
            pltpu.VMEM((256, OPS * SITES), BF16),
            pltpu.VMEM((2, SITES, 128), F32),
            pltpu.VMEM((4, SITES, 128), F32),
            pltpu.VMEM((128, SITES), F32),
            pltpu.VMEM((2, SITES, 128), F32),
            pltpu.VMEM((128, SITES), F32),
            pltpu.VMEM((128, SITES), F32),
            pltpu.VMEM((8, 128, SITES), F32),
            pltpu.VMEM((4, 128, SITES), F32),
            pltpu.VMEM((COUNT_B, 8, 128), F32),
            dma((4, PLANE)),
            dma((4, PLANE)),
            dma((4, 4)),
            dma((4, 4)),
            dma((4,)),
            dma((4,)),
            dma((14,)),
            dma((14,)),
        ],
        compiler_params=pltpu.CompilerParams(
            collective_id=0, has_side_effects=True, vmem_limit_bytes=48 << 20
        ),
    )(par, start, operators, keep)
    return result.reshape(2, ROWS, SITES).transpose(1, 0, 2).reshape(density.shape)


def solution(mesh):
    placed = (
        P("rows", "occa", "occb", None, None),
        P(None, "rows", None),
        P(),
        P(),
        P("occa", "occb"),
    )
    return jax.shard_map(
        shards,
        mesh=mesh,
        in_specs=placed,
        out_specs=P("rows", "occa", "occb", None, None),
        check_vma=False,
    )
```

```python
import math
import jax
import jax.numpy as jnp
from jax import lax
from jax.experimental import pallas as pl
from jax.experimental.pallas import tpu as pltpu
from jax.sharding import PartitionSpec as P

TIME_STEP = 0.05
MESH = pl.DeviceIdType.MESH
F32 = jnp.float32
BF16 = jnp.bfloat16
SITES = 512
OPS = 5
ROWS = 64
COLS = 16
PLANE = 32
COUNT_A = 8
COUNT_B = 4


def split(value):
    high = value.astype(BF16)
    low = (value - high.astype(F32)).astype(BF16)
    return high, low


def root(count):
    value = jnp.float32(0.0)
    for n in range(1, COUNT_A):
        value = jnp.where(count == n, math.sqrt(n), value)
    return value


def kernel(
    rates, coupling, mask, density, ops, out,
    dens, own, oth, whi, wlo, ghl,
    sent_r, cols_buf, held_c, pack, first_r, first_c,
    near_r, near_c, keeps,
    a_send, a_recv, n_send, n_recv, k_send, k_recv, o_send, o_recv,
):
    ia = lax.axis_index("occa")
    ib = lax.axis_index("occb")
    ir = lax.axis_index("rows")
    half = ir // 4
    iy = lax.rem(ir, 4)
    ix = ia // 2
    core = lax.rem(ia, 2)
    iz = half * 4 + ib
    me_col = iz * 4 + iy
    me_row = ib * 8 + ir

    def a_dev(step):
        return {"occa": lax.rem(ia + step + COUNT_A, COUNT_A)}

    def z_dev(step):
        z = lax.rem(iz + step + 8, 8)
        return {"occb": lax.rem(z, 4), "rows": (z // 4) * 4 + iy}

    def y_dev(step):
        return {"rows": half * 4 + lax.rem(iy + step, 4)}

    def partner(j):
        z = lax.rem(iz + j // 4, 8)
        y = lax.rem(iy + lax.rem(j, 4), 4)
        b = lax.rem(z, 4)
        r = (z // 4) * 4 + y
        return {"occb": b, "rows": r}, z * 4 + y, b * 8 + r

    barrier = pltpu.get_barrier_semaphore()

    def greet(j, carry):
        pl.semaphore_signal(barrier, inc=1, device_id=partner(j)[0], device_id_type=MESH)
        return carry

    lax.fori_loop(1, PLANE, greet, 0)
    for step in (1, -1, 2, -2, 4):
        pl.semaphore_signal(barrier, inc=1, device_id=a_dev(step), device_id_type=MESH)

    kept = mask[0, 0].astype(F32)
    for part in range(2):
        dens[part * ROWS:(part + 1) * ROWS, :] = kept * density[:, part, :]
    sent_r[0] = dens[...].T
    keeps[ib] = jnp.full((8, 128), kept, F32)
    down_a = root(ia)
    up_a = jnp.where(ia < COUNT_A - 1, root(ia + 1), 0.0)
    damp = ia.astype(F32) * rates[0] + ib.astype(F32) * rates[1]

    def factors(b):
        down_b = root(b)
        up_b = jnp.where(b < COUNT_B - 1, root(b + 1), 0.0)
        return [
            (0.0, -1.0),
            (0.0, -up_a),
            (down_a * coupling[0, 1], -down_a * coupling[0, 0]),
            (0.0, -up_b),
            (down_b * coupling[1, 1], -down_b * coupling[1, 0]),
        ]

    sibling = {"occa": ix * 2 + 1 - core}

    def remote(src, dst, send, recv, dev):
        return pltpu.make_async_remote_copy(
            src_ref=src, dst_ref=dst, send_sem=send, recv_sem=recv, device_id=dev, device_id_type=MESH
        )

    def block(index):
        return pl.ds(pl.multiple_of(index * COLS, COLS), COLS)

    def to_columns(slot, j):
        dev, col, row = partner(j)
        return remote(sent_r.at[slot, block(col)], cols_buf.at[slot, block(me_row)],
                      a_send.at[slot, j], a_recv.at[slot, me_row], dev)

    def to_rows(slot, j):
        dev, col, row = partner(j)
        return remote(pack.at[slot - 2, block(row)], cols_buf.at[slot, block(me_col)],
                      a_send.at[slot, j], a_recv.at[slot, me_col], dev)

    def start_columns(slot):
        def body(j, carry):
            to_columns(slot, j).start()
            return carry
        lax.fori_loop(1, PLANE, body, 0)
        cols_buf[slot, block(me_row), :] = sent_r[slot, block(me_col), :]

    def start_rows(slot):
        def body(j, carry):
            to_rows(slot, j).start()
            return carry
        lax.fori_loop(1, PLANE, body, 0)
        cols_buf[slot, block(me_col), :] = pack[slot - 2, block(me_row), :]

    def finish_recv(slot, by_row):
        def body(j, carry):
            dev, col, row = partner(j)
            index = row if by_row else col
            piece = cols_buf.at[slot, block(index)]
            remote(piece, piece, a_send.at[slot, j], a_recv.at[slot, index], dev).wait_recv()
            return carry
        lax.fori_loop(1, PLANE, body, 0)

    def finish_send(slot):
        def body(j, carry):
            (to_columns if slot < 2 else to_rows)(slot, j).wait_send()
            return carry
        lax.fori_loop(1, PLANE, body, 0)

    lanes = lax.broadcasted_iota(jnp.int32, (COLS, 128), 1) < 64

    def unpack(slot):
        parts = []
        for b in range(COUNT_B):
            real, imag = [], []
            for t in range(4):
                q = (b * 8 + 2 * t) * COLS
                even = cols_buf[slot, q:q + COLS, :]
                odd = cols_buf[slot, q + COLS:q + 2 * COLS, :]
                real.append(jnp.where(lanes, even, pltpu.roll(odd, 64, 1)))
                imag.append(jnp.where(lanes, pltpu.roll(even, 64, 1), odd))
            parts.append(jnp.concatenate(real, axis=1))
            parts.append(jnp.concatenate(imag, axis=1))
        return jnp.concatenate(parts, axis=0)

    def repack(slot, value):
        for b in range(COUNT_B):
            for t in range(4):
                real = value[32 * b:32 * b + COLS, 128 * t:128 * t + 128]
                imag = value[32 * b + COLS:32 * b + 32, 128 * t:128 * t + 128]
                q = (b * 8 + 2 * t) * COLS
                pack[slot - 2, q:q + COLS, :] = jnp.where(lanes, real, pltpu.roll(imag, 64, 1))
                pack[slot - 2, q + COLS:q + 2 * COLS, :] = jnp.where(lanes, pltpu.roll(real, 64, 1), imag)

    def put(k, row, value):
        high, low = split(value)
        count = value.shape[0]
        ghl[row:row + count, k * SITES:(k + 1) * SITES] = high
        ghl[128 + row:128 + row + count, k * SITES:(k + 1) * SITES] = low

    def multiply():
        both = jnp.dot(ghl[...], whi[...], preferred_element_type=F32)
        rest = jnp.dot(ghl[0:128, :], wlo[...], preferred_element_type=F32)
        return both[0:128] + both[128:256] + rest

    def right(center, base):
        fields = [center, near_r.at[base], near_r.at[base + 1], near_r.at[base + 2], near_r.at[base + 3]]
        own_factors = factors(ib)
        for k, field in enumerate(fields):
            re, im = field[0:ROWS, :], field[ROWS:128, :]
            f_re, f_im = own_factors[k]
            put(k, 0, f_re * re + f_im * im)
            put(k, ROWS, f_re * im - f_im * re)
        return multiply()

    def left(center, base):
        for b in range(COUNT_B):
            b_factors = factors(b)
            for k in range(OPS):
                source, at = center, b
                if k == 1:
                    source = near_c.at[base]
                elif k == 2:
                    source = near_c.at[base + 1]
                elif k == 3:
                    at = min(b + 1, COUNT_B - 1)
                elif k == 4:
                    at = max(b - 1, 0)
                re = source[32 * at:32 * at + COLS, :]
                im = source[32 * at + COLS:32 * at + 32, :]
                f_re, f_im = b_factors[k]
                put(k, 32 * b, f_re * re - f_im * im)
                put(k, 32 * b + COLS, f_re * im + f_im * re)
        return multiply()

    def near_copy(kind, index, src, dst, dev):
        return remote(src, dst, n_send.at[kind, index], n_recv.at[kind, index], dev)

    def row_moves(kind, src):
        base = 4 * kind
        return [
            near_copy(kind, 0, src, near_r.at[base], a_dev(-1)),
            near_copy(kind, 1, src, near_r.at[base + 1], a_dev(1)),
            near_copy(kind, 2, src, near_r.at[base + 2], z_dev(-1)),
            near_copy(kind, 3, src, near_r.at[base + 3], z_dev(1)),
        ]

    def col_moves(kind, src):
        base = 2 * kind
        return [
            near_copy(2 + kind, 0, src, near_c.at[base], a_dev(-1)),
            near_copy(2 + kind, 1, src, near_c.at[base + 1], a_dev(1)),
        ]

    def eight(index):
        return pl.ds(pl.multiple_of(index * 8, 8), 8)

    def thirty_two(index):
        return pl.ds(pl.multiple_of(index * 32, 32), 32)

    def wide(index):
        return pl.ds(pl.multiple_of(index * 256, 256), 256)

    share = core * 4 + ix
    half_z = remote(ops.at[:, eight(share), wide(half)], oth.at[iy, :, eight(share), :],
                    o_send.at[0], o_recv.at[0], z_dev(4))
    half_y = [remote(oth.at[iy, :, eight(share), :], oth.at[iy, :, eight(share), :],
                     o_send.at[s], o_recv.at[s], y_dev(s)) for s in (1, 2, 3)]
    half_x = [remote(oth.at[:, :, eight(share), :], oth.at[:, :, eight(share), :],
                     o_send.at[3 + s], o_recv.at[3 + s], a_dev(2 * s)) for s in (1, 2, 3)]
    half_c = remote(oth.at[:, :, thirty_two(core), :], oth.at[:, :, thirty_two(core), :],
                    o_send.at[7], o_recv.at[7], sibling)
    own_y = [remote(ops.at[:, thirty_two(core), :], own.at[iy, :, thirty_two(core), :],
                    o_send.at[8 + n], o_recv.at[8 + n], y_dev((1, 3)[n])) for n in range(2)]

    def held(n, rows):
        return own.at[lax.rem(iy + (3, 1, 2)[n], 4), :, rows, :]

    def sixteen(index):
        return pl.ds(pl.multiple_of(index * 16, 16), 16)

    passed = [remote(held(n, sixteen(2 * core + n)), held(n, sixteen(2 * core + n)),
                     o_send.at[10 + n], o_recv.at[10 + n], y_dev((1, 3)[n])) for n in range(2)]

    def own_c(n):
        return remote(held(n, thirty_two(core)), held(n, thirty_two(core)),
                      o_send.at[12 + n], o_recv.at[12 + n], sibling)

    keep_moves = [remote(keeps.at[ib], keeps.at[ib], k_send.at[s], k_recv.at[s],
                         {"occb": lax.rem(ib + s, COUNT_B)}) for s in (1, 2, 3)]

    pl.semaphore_wait(barrier, PLANE - 1 + 5)
    half_z.start()
    start_columns(0)
    for copy in own_y:
        copy.start()
    start_moves = row_moves(0, dens)
    for copy in keep_moves + start_moves:
        copy.start()

    def put_operator(y, rows):
        for k in range(OPS):
            at = pl.ds(pl.multiple_of(k * SITES + half * 256 + y * ROWS, ROWS), ROWS)
            high, low = split(rows[k])
            whi[at, :] = high
            wlo[at, :] = low

    half_z.wait_recv()
    for copy in half_y:
        copy.start()
    put_operator(iy, ops)
    own_moves = []
    for n in range(2):
        own_y[n].wait_recv()
        passed[n].start()
        own_moves.append(own_c(n))
        own_moves[n].start()
    for copy in half_y:
        copy.wait_recv()
    for copy in half_x:
        copy.start()

    finish_recv(0, True)
    held_c[...] = unpack(0)
    start_cols = col_moves(0, held_c)
    for copy in start_cols:
        copy.start()

    for copy in passed:
        copy.wait_recv()
    own_moves.append(own_c(2))
    own_moves[2].start()
    for n in range(3):
        own_moves[n].wait_recv()
        put_operator(lax.rem(iy + (3, 1, 2)[n], 4), own.at[lax.rem(iy + (3, 1, 2)[n], 4)])
    for k in range(OPS):
        source = pl.ds(pl.multiple_of(k * SITES + half * 256, 256), 256)
        target = pl.ds(pl.multiple_of(k * SITES + (1 - half) * 256, 256), 256)
        whi[target, wide(half)] = whi[source, wide(1 - half)].T
        wlo[target, wide(half)] = wlo[source, wide(1 - half)].T
    for copy in half_x:
        copy.wait_recv()
    half_c.start()
    half_c.wait_recv()
    for k in range(OPS):
        for y in range(4):
            at = pl.ds(pl.multiple_of(k * SITES + (1 - half) * 256 + y * ROWS, ROWS), ROWS)
            high, low = split(oth[y, k])
            whi[at, wide(1 - half)] = high
            wlo[at, wide(1 - half)] = low

    for copy in start_moves:
        copy.wait_recv()
    first_r[...] = kept * (right(dens, 0) - damp * dens[...])
    sent_r[1] = first_r[...].T
    start_columns(1)

    for copy in start_cols:
        copy.wait_recv()
    for copy in keep_moves:
        copy.wait_recv()
    kept_c = jnp.concatenate(
        [jnp.broadcast_to(keeps[b, 0:1, 0:1], (2 * COLS, SITES)) for b in range(COUNT_B)], axis=0
    )
    first_c[...] = kept_c * left(held_c, 0)
    repack(2, first_c[...])
    start_rows(2)

    finish_recv(1, True)
    first_c[...] += unpack(1)
    next_cols = col_moves(1, first_c)
    for copy in next_cols:
        copy.start()
    finish_recv(2, False)
    first_r[...] += cols_buf[2].T
    next_moves = row_moves(1, first_r)
    for copy in next_moves:
        copy.start()

    for copy in next_cols:
        copy.wait_recv()
    repack(3, left(first_c, 2))
    start_rows(3)

    for copy in next_moves:
        copy.wait_recv()
    second = right(first_r, 4) - damp * first_r[...]
    finish_recv(3, False)
    second = kept * (second + cols_buf[3].T)
    result = dens[...] + TIME_STEP * first_r[...] + (0.5 * TIME_STEP * TIME_STEP) * second
    for part in range(2):
        out[:, part, :] = result[part * ROWS:(part + 1) * ROWS]

    for copy in [half_z, half_c] + half_y + half_x + passed:
        copy.wait_send()
    for slot in range(4):
        finish_send(slot)
    for copy in keep_moves + own_y + own_moves + start_moves + start_cols + next_cols + next_moves:
        copy.wait_send()


def shards(density, operators, rates, coupling, keep_mask):
    vmem = pl.BlockSpec(memory_space=pltpu.VMEM)
    smem = pl.BlockSpec(memory_space=pltpu.SMEM)
    dma = pltpu.SemaphoreType.DMA
    result = pl.pallas_call(
        kernel,
        out_shape=jax.ShapeDtypeStruct((ROWS, 2, SITES), F32),
        in_specs=[smem, smem, smem, vmem, vmem],
        out_specs=vmem,
        scratch_shapes=[
            pltpu.VMEM((2 * ROWS, SITES), F32),
            pltpu.VMEM((4, OPS, ROWS, SITES), F32),
            pltpu.VMEM((4, OPS, ROWS, SITES // 2), F32),
            pltpu.VMEM((OPS * SITES, SITES), BF16),
            pltpu.VMEM((OPS * SITES, SITES), BF16),
            pltpu.VMEM((256, OPS * SITES), BF16),
            pltpu.VMEM((2, SITES, 128), F32),
            pltpu.VMEM((4, SITES, 128), F32),
            pltpu.VMEM((128, SITES), F32),
            pltpu.VMEM((2, SITES, 128), F32),
            pltpu.VMEM((128, SITES), F32),
            pltpu.VMEM((128, SITES), F32),
            pltpu.VMEM((8, 128, SITES), F32),
            pltpu.VMEM((4, 128, SITES), F32),
            pltpu.VMEM((COUNT_B, 8, 128), F32),
            dma((4, PLANE)),
            dma((4, PLANE)),
            dma((4, 4)),
            dma((4, 4)),
            dma((4,)),
            dma((4,)),
            dma((15,)),
            dma((15,)),
        ],
        compiler_params=pltpu.CompilerParams(
            collective_id=0, has_side_effects=True, vmem_limit_bytes=48 << 20
        ),
    )(rates, coupling, keep_mask, density.reshape(ROWS, 2, SITES), operators)
    return result.reshape(density.shape)


def solution(mesh):
    placed = (
        P("rows", "occa", "occb", None, None),
        P(None, "rows", None),
        P(),
        P(),
        P("occa", "occb"),
    )
    return jax.shard_map(
        shards,
        mesh=mesh,
        in_specs=placed,
        out_specs=P("rows", "occa", "occb", None, None),
        check_vma=False,
    )
```

```python
import math
import jax
import jax.numpy as jnp
from jax import lax
from jax.experimental import pallas as pl
from jax.experimental.pallas import tpu as pltpu
from jax.sharding import PartitionSpec as P

TIME_STEP = 0.05
MESH = pl.DeviceIdType.MESH
F32 = jnp.float32
BF16 = jnp.bfloat16
SITES = 512
OPS = 5
ROWS = 64
COLS = 16
PLANE = 32
COUNT_A = 8
COUNT_B = 4


def split(value):
    high = value.astype(BF16)
    low = (value - high.astype(F32)).astype(BF16)
    return high, low


def root(count):
    value = jnp.float32(0.0)
    for n in range(1, COUNT_A):
        value = jnp.where(count == n, math.sqrt(n), value)
    return value


def kernel(
    rates, coupling, mask, density_in, ops_in, out,
    density, ops, dens, own, oth, whi, wlo, ghl,
    sent_r, cols_buf, held_c, pack, first_r, first_c,
    near_r, near_c, keeps,
    a_send, a_recv, n_send, n_recv, k_send, k_recv, o_send, o_recv, l_sem,
):
    ia = lax.axis_index("occa")
    ib = lax.axis_index("occb")
    ir = lax.axis_index("rows")
    half = ir // 4
    iy = lax.rem(ir, 4)
    ix = ia // 2
    core = lax.rem(ia, 2)
    iz = half * 4 + ib
    me_col = iz * 4 + iy
    me_row = ib * 8 + ir

    def a_dev(step):
        return {"occa": lax.rem(ia + step + COUNT_A, COUNT_A)}

    def z_dev(step):
        z = lax.rem(iz + step + 8, 8)
        return {"occb": lax.rem(z, 4), "rows": (z // 4) * 4 + iy}

    def y_dev(step):
        return {"rows": half * 4 + lax.rem(iy + step, 4)}

    def partner(j):
        turn = j // 4
        quarter = lax.rem(j, 4)
        away = 4 + jnp.where(lax.rem(turn, 2) == 1, -((turn + 1) // 2), turn // 2)
        aside = jnp.where(quarter < 2, 2 - quarter, jnp.where(quarter == 2, 3, 0))
        z = lax.rem(iz + away, 8)
        y = lax.rem(iy + aside, 4)
        b = lax.rem(z, 4)
        r = (z // 4) * 4 + y
        return {"occb": b, "rows": r}, z * 4 + y, b * 8 + r

    barrier = pltpu.get_barrier_semaphore()

    def greet(j, carry):
        pl.semaphore_signal(barrier, inc=1, device_id=partner(j)[0], device_id_type=MESH)
        return carry

    lax.fori_loop(0, PLANE - 1, greet, 0)
    for step in (1, -1, 2, -2, 4):
        pl.semaphore_signal(barrier, inc=1, device_id=a_dev(step), device_id_type=MESH)

    load_density = pltpu.make_async_copy(density_in, density, l_sem.at[0])
    load_ops = pltpu.make_async_copy(ops_in, ops, l_sem.at[1])
    load_density.start()
    load_ops.start()
    load_density.wait()
    kept = mask[0, 0].astype(F32)
    for part in range(2):
        dens[part * ROWS:(part + 1) * ROWS, :] = kept * density[:, part, :]
    sent_r[0] = dens[...].T
    keeps[ib] = jnp.full((8, 128), kept, F32)
    down_a = root(ia)
    up_a = jnp.where(ia < COUNT_A - 1, root(ia + 1), 0.0)
    damp = ia.astype(F32) * rates[0] + ib.astype(F32) * rates[1]

    def factors(b):
        down_b = root(b)
        up_b = jnp.where(b < COUNT_B - 1, root(b + 1), 0.0)
        return [
            (0.0, -1.0),
            (0.0, -up_a),
            (down_a * coupling[0, 1], -down_a * coupling[0, 0]),
            (0.0, -up_b),
            (down_b * coupling[1, 1], -down_b * coupling[1, 0]),
        ]

    sibling = {"occa": ix * 2 + 1 - core}

    def remote(src, dst, send, recv, dev):
        return pltpu.make_async_remote_copy(
            src_ref=src, dst_ref=dst, send_sem=send, recv_sem=recv, device_id=dev, device_id_type=MESH
        )

    def block(index):
        return pl.ds(pl.multiple_of(index * COLS, COLS), COLS)

    def to_columns(slot, j):
        dev, col, row = partner(j)
        return remote(sent_r.at[slot, block(col)], cols_buf.at[slot, block(me_row)],
                      a_send.at[slot, j], a_recv.at[slot, me_row], dev)

    def to_rows(slot, j):
        dev, col, row = partner(j)
        return remote(pack.at[slot - 2, block(row)], cols_buf.at[slot, block(me_col)],
                      a_send.at[slot, j], a_recv.at[slot, me_col], dev)

    def start_columns(slot):
        def body(j, carry):
            to_columns(slot, j).start()
            return carry
        lax.fori_loop(0, PLANE - 1, body, 0)
        cols_buf[slot, block(me_row), :] = sent_r[slot, block(me_col), :]

    def start_rows(slot):
        def body(j, carry):
            to_rows(slot, j).start()
            return carry
        lax.fori_loop(0, PLANE - 1, body, 0)
        cols_buf[slot, block(me_col), :] = pack[slot - 2, block(me_row), :]

    def finish_recv(slot, by_row):
        def body(j, carry):
            dev, col, row = partner(j)
            index = row if by_row else col
            piece = cols_buf.at[slot, block(index)]
            remote(piece, piece, a_send.at[slot, j], a_recv.at[slot, index], dev).wait_recv()
            return carry
        lax.fori_loop(0, PLANE - 1, body, 0)

    def finish_send(slot):
        def body(j, carry):
            (to_columns if slot < 2 else to_rows)(slot, j).wait_send()
            return carry
        lax.fori_loop(0, PLANE - 1, body, 0)

    lanes = lax.broadcasted_iota(jnp.int32, (COLS, 128), 1) < 64

    def unpack(slot):
        parts = []
        for b in range(COUNT_B):
            real, imag = [], []
            for t in range(4):
                q = (b * 8 + 2 * t) * COLS
                even = cols_buf[slot, q:q + COLS, :]
                odd = cols_buf[slot, q + COLS:q + 2 * COLS, :]
                real.append(jnp.where(lanes, even, pltpu.roll(odd, 64, 1)))
                imag.append(jnp.where(lanes, pltpu.roll(even, 64, 1), odd))
            parts.append(jnp.concatenate(real, axis=1))
            parts.append(jnp.concatenate(imag, axis=1))
        return jnp.concatenate(parts, axis=0)

    def repack(slot, value):
        for b in range(COUNT_B):
            for t in range(4):
                real = value[32 * b:32 * b + COLS, 128 * t:128 * t + 128]
                imag = value[32 * b + COLS:32 * b + 32, 128 * t:128 * t + 128]
                q = (b * 8 + 2 * t) * COLS
                pack[slot - 2, q:q + COLS, :] = jnp.where(lanes, real, pltpu.roll(imag, 64, 1))
                pack[slot - 2, q + COLS:q + 2 * COLS, :] = jnp.where(lanes, pltpu.roll(real, 64, 1), imag)

    def put(k, row, value):
        high, low = split(value)
        count = value.shape[0]
        ghl[row:row + count, k * SITES:(k + 1) * SITES] = high
        ghl[128 + row:128 + row + count, k * SITES:(k + 1) * SITES] = low

    def multiply():
        both = jnp.dot(ghl[...], whi[...], preferred_element_type=F32)
        rest = jnp.dot(ghl[0:128, :], wlo[...], preferred_element_type=F32)
        return both[0:128] + both[128:256] + rest

    def right(center, base):
        fields = [center, near_r.at[base], near_r.at[base + 1], near_r.at[base + 2], near_r.at[base + 3]]
        own_factors = factors(ib)
        for k, field in enumerate(fields):
            re, im = field[0:ROWS, :], field[ROWS:128, :]
            f_re, f_im = own_factors[k]
            put(k, 0, f_re * re + f_im * im)
            put(k, ROWS, f_re * im - f_im * re)
        return multiply()

    def left(center, base):
        for b in range(COUNT_B):
            b_factors = factors(b)
            for k in range(OPS):
                source, at = center, b
                if k == 1:
                    source = near_c.at[base]
                elif k == 2:
                    source = near_c.at[base + 1]
                elif k == 3:
                    at = min(b + 1, COUNT_B - 1)
                elif k == 4:
                    at = max(b - 1, 0)
                re = source[32 * at:32 * at + COLS, :]
                im = source[32 * at + COLS:32 * at + 32, :]
                f_re, f_im = b_factors[k]
                put(k, 32 * b, f_re * re - f_im * im)
                put(k, 32 * b + COLS, f_re * im + f_im * re)
        return multiply()

    def near_copy(kind, index, src, dst, dev):
        return remote(src, dst, n_send.at[kind, index], n_recv.at[kind, index], dev)

    def row_moves(kind, src):
        base = 4 * kind
        return [
            near_copy(kind, 0, src, near_r.at[base], a_dev(-1)),
            near_copy(kind, 1, src, near_r.at[base + 1], a_dev(1)),
            near_copy(kind, 2, src, near_r.at[base + 2], z_dev(-1)),
            near_copy(kind, 3, src, near_r.at[base + 3], z_dev(1)),
        ]

    def col_moves(kind, src):
        base = 2 * kind
        return [
            near_copy(2 + kind, 0, src, near_c.at[base], a_dev(-1)),
            near_copy(2 + kind, 1, src, near_c.at[base + 1], a_dev(1)),
        ]

    def eight(index):
        return pl.ds(pl.multiple_of(index * 8, 8), 8)

    def thirty_two(index):
        return pl.ds(pl.multiple_of(index * 32, 32), 32)

    def wide(index):
        return pl.ds(pl.multiple_of(index * 256, 256), 256)

    share = core * 4 + ix
    half_z = remote(ops.at[:, eight(share), wide(half)], oth.at[iy, :, eight(share), :],
                    o_send.at[0], o_recv.at[0], z_dev(4))
    half_y = [remote(oth.at[iy, :, eight(share), :], oth.at[iy, :, eight(share), :],
                     o_send.at[s], o_recv.at[s], y_dev(s)) for s in (1, 2, 3)]
    half_x = [remote(oth.at[:, :, eight(share), :], oth.at[:, :, eight(share), :],
                     o_send.at[3 + s], o_recv.at[3 + s], a_dev(2 * s)) for s in (1, 2, 3)]
    def half_c(s):
        rows = eight(core * 4 + lax.rem(ix + 4 - s, 4))
        return remote(oth.at[:, :, rows, :], oth.at[:, :, rows, :],
                      o_send.at[7 + s], o_recv.at[7 + s], sibling)

    def own_y(part, n):
        cols = slice(256 * part, 256 * part + 256)
        return remote(ops.at[:, thirty_two(core), cols], own.at[iy, :, thirty_two(core), cols],
                      o_send.at[11 + 2 * part + n], o_recv.at[11 + 2 * part + n], y_dev((1, 3)[n]))

    own_one = [own_y(0, n) for n in range(2)]
    own_two = [own_y(1, n) for n in range(2)]

    def held(n, rows):
        return own.at[lax.rem(iy + (3, 1, 2)[n], 4), :, rows, :]

    def sixteen(index):
        return pl.ds(pl.multiple_of(index * 16, 16), 16)

    passed = [remote(held(n, sixteen(2 * core + n)), held(n, sixteen(2 * core + n)),
                     o_send.at[15 + n], o_recv.at[15 + n], y_dev((1, 3)[n])) for n in range(2)]

    def own_c(n):
        return remote(held(n, thirty_two(core)), held(n, thirty_two(core)),
                      o_send.at[17 + n], o_recv.at[17 + n], sibling)

    keep_moves = [remote(keeps.at[ib], keeps.at[ib], k_send.at[s], k_recv.at[s],
                         {"occb": lax.rem(ib + s, COUNT_B)}) for s in (1, 2, 3)]

    load_ops.wait()
    pl.semaphore_wait(barrier, PLANE - 1 + 5)
    half_z.start()
    start_columns(0)
    for copy in own_one:
        copy.start()
    start_moves = row_moves(0, dens)
    for copy in keep_moves + start_moves:
        copy.start()

    def put_operator(y, rows):
        for k in range(OPS):
            at = pl.ds(pl.multiple_of(k * SITES + half * 256 + y * ROWS, ROWS), ROWS)
            high, low = split(rows[k])
            whi[at, :] = high
            wlo[at, :] = low

    half_z.wait_recv()
    for copy in half_y + own_two:
        copy.start()
    put_operator(iy, ops)
    for copy in half_y:
        copy.wait_recv()
    half_moves = [half_c(0)]
    for copy in half_x + half_moves:
        copy.start()

    finish_recv(0, True)
    held_c[...] = unpack(0)
    start_cols = col_moves(0, held_c)
    for copy in start_cols:
        copy.start()

    own_moves = []
    for n in range(2):
        own_one[n].wait_recv()
        own_two[n].wait_recv()
        passed[n].start()
        own_moves.append(own_c(n))
        own_moves[n].start()
    for n in range(2):
        own_moves[n].wait_recv()
        put_operator(lax.rem(iy + (3, 1)[n], 4), own.at[lax.rem(iy + (3, 1)[n], 4)])
    for copy in passed:
        copy.wait_recv()
    own_moves.append(own_c(2))
    own_moves[2].start()
    own_moves[2].wait_recv()
    put_operator(lax.rem(iy + 2, 4), own.at[lax.rem(iy + 2, 4)])
    for k in range(OPS):
        source = pl.ds(pl.multiple_of(k * SITES + half * 256, 256), 256)
        target = pl.ds(pl.multiple_of(k * SITES + (1 - half) * 256, 256), 256)
        whi[target, wide(half)] = whi[source, wide(1 - half)].T
        wlo[target, wide(half)] = wlo[source, wide(1 - half)].T
    for s in (1, 3, 2):
        half_x[s - 1].wait_recv()
        half_moves.append(half_c(s))
        half_moves[-1].start()
    for copy in half_moves:
        copy.wait_recv()
    for k in range(OPS):
        for y in range(4):
            at = pl.ds(pl.multiple_of(k * SITES + (1 - half) * 256 + y * ROWS, ROWS), ROWS)
            high, low = split(oth[y, k])
            whi[at, wide(1 - half)] = high
            wlo[at, wide(1 - half)] = low

    for copy in start_moves:
        copy.wait_recv()
    first_r[...] = kept * (right(dens, 0) - damp * dens[...])
    sent_r[1] = first_r[...].T
    start_columns(1)

    for copy in start_cols:
        copy.wait_recv()
    for copy in keep_moves:
        copy.wait_recv()
    kept_c = jnp.concatenate(
        [jnp.broadcast_to(keeps[b, 0:1, 0:1], (2 * COLS, SITES)) for b in range(COUNT_B)], axis=0
    )
    first_c[...] = kept_c * left(held_c, 0)
    repack(2, first_c[...])
    start_rows(2)

    finish_recv(1, True)
    first_c[...] += unpack(1)
    next_cols = col_moves(1, first_c)
    for copy in next_cols:
        copy.start()
    finish_recv(2, False)
    first_r[...] += cols_buf[2].T
    next_moves = row_moves(1, first_r)
    for copy in next_moves:
        copy.start()

    for copy in next_cols:
        copy.wait_recv()
    repack(3, left(first_c, 2))
    start_rows(3)

    for copy in next_moves:
        copy.wait_recv()
    second = right(first_r, 4) - damp * first_r[...]
    finish_recv(3, False)
    second = kept * (second + cols_buf[3].T)
    result = dens[...] + TIME_STEP * first_r[...] + (0.5 * TIME_STEP * TIME_STEP) * second
    for part in range(2):
        out[:, part, :] = result[part * ROWS:(part + 1) * ROWS]

    for copy in [half_z] + half_y + half_x + half_moves + passed + own_one + own_two:
        copy.wait_send()
    for slot in range(4):
        finish_send(slot)
    for copy in keep_moves + own_moves + start_moves + start_cols + next_cols + next_moves:
        copy.wait_send()


def shards(density, operators, rates, coupling, keep_mask):
    vmem = pl.BlockSpec(memory_space=pltpu.VMEM)
    smem = pl.BlockSpec(memory_space=pltpu.SMEM)
    hbm = pl.BlockSpec(memory_space=pl.ANY)
    dma = pltpu.SemaphoreType.DMA
    result = pl.pallas_call(
        kernel,
        out_shape=jax.ShapeDtypeStruct((ROWS, 2, SITES), F32),
        in_specs=[smem, smem, smem, hbm, hbm],
        out_specs=vmem,
        scratch_shapes=[
            pltpu.VMEM((ROWS, 2, SITES), F32),
            pltpu.VMEM((OPS, ROWS, SITES), F32),
            pltpu.VMEM((2 * ROWS, SITES), F32),
            pltpu.VMEM((4, OPS, ROWS, SITES), F32),
            pltpu.VMEM((4, OPS, ROWS, SITES // 2), F32),
            pltpu.VMEM((OPS * SITES, SITES), BF16),
            pltpu.VMEM((OPS * SITES, SITES), BF16),
            pltpu.VMEM((256, OPS * SITES), BF16),
            pltpu.VMEM((2, SITES, 128), F32),
            pltpu.VMEM((4, SITES, 128), F32),
            pltpu.VMEM((128, SITES), F32),
            pltpu.VMEM((2, SITES, 128), F32),
            pltpu.VMEM((128, SITES), F32),
            pltpu.VMEM((128, SITES), F32),
            pltpu.VMEM((8, 128, SITES), F32),
            pltpu.VMEM((4, 128, SITES), F32),
            pltpu.VMEM((COUNT_B, 8, 128), F32),
            dma((4, PLANE)),
            dma((4, PLANE)),
            dma((4, 4)),
            dma((4, 4)),
            dma((4,)),
            dma((4,)),
            dma((20,)),
            dma((20,)),
            dma((2,)),
        ],
        compiler_params=pltpu.CompilerParams(
            collective_id=0, has_side_effects=True, vmem_limit_bytes=60 << 20
        ),
    )(rates, coupling, keep_mask, density.reshape(ROWS, 2, SITES), operators)
    return result.reshape(density.shape)


def solution(mesh):
    placed = (
        P("rows", "occa", "occb", None, None),
        P(None, "rows", None),
        P(),
        P(),
        P("occa", "occb"),
    )
    return jax.shard_map(
        shards,
        mesh=mesh,
        in_specs=placed,
        out_specs=P("rows", "occa", "occb", None, None),
        check_vma=False,
    )
```

```python
import math
import jax
import jax.numpy as jnp
from jax import lax
from jax.experimental import pallas as pl
from jax.experimental.pallas import tpu as pltpu
from jax.sharding import PartitionSpec as P

TIME_STEP = 0.05
MESH = pl.DeviceIdType.MESH
F32 = jnp.float32
BF16 = jnp.bfloat16
SITES = 512
OPS = 5
ROWS = 64
COLS = 16
PLANE = 32
COUNT_A = 8
COUNT_B = 4


def split(value):
    high = value.astype(BF16)
    low = (value - high.astype(F32)).astype(BF16)
    return high, low


def root(count):
    value = jnp.float32(0.0)
    for n in range(1, COUNT_A):
        value = jnp.where(count == n, math.sqrt(n), value)
    return value


def kernel(
    rates_in, coupling_in, mask, density_in, ops_in, out,
    rates, coupling, density, ops, dens, own, oth, whi, wlo, ghl,
    sent_r, cols_buf, held_c, pack, first_r, first_c,
    near_r, near_c, keeps,
    a_send, a_recv, n_send, n_recv, k_send, k_recv, o_send, o_recv, l_sem,
):
    ia = lax.axis_index("occa")
    ib = lax.axis_index("occb")
    ir = lax.axis_index("rows")
    half = ir // 4
    iy = lax.rem(ir, 4)
    ix = ia // 2
    core = lax.rem(ia, 2)
    iz = half * 4 + ib
    me_col = iz * 4 + iy
    me_row = ib * 8 + ir

    far, near = 1 - half, half

    def a_dev(step):
        return {"occa": lax.rem(ia + step + COUNT_A, COUNT_A)}

    def z_dev(step):
        z = lax.rem(iz + step + 8, 8)
        return {"occb": lax.rem(z, 4), "rows": (z // 4) * 4 + iy}

    def y_dev(step):
        return {"rows": half * 4 + lax.rem(iy + step, 4)}

    def partner(j):
        turn = j // 4
        quarter = lax.rem(j, 4)
        away = 4 + jnp.where(lax.rem(turn, 2) == 1, -((turn + 1) // 2), turn // 2)
        aside = jnp.where(quarter < 2, 2 - quarter, jnp.where(quarter == 2, 3, 0))
        z = lax.rem(iz + away, 8)
        y = lax.rem(iy + aside, 4)
        b = lax.rem(z, 4)
        r = (z // 4) * 4 + y
        return {"occb": b, "rows": r}, z * 4 + y, b * 8 + r

    def half_partner(j):
        turn = lax.rem(j // 4, 4)
        quarter = lax.rem(j, 4)
        aside = jnp.where(quarter < 2, 2 - quarter, jnp.where(quarter == 2, 3, 0))
        b = lax.rem(ib + jnp.where(j < 16, turn, 3 - turn), COUNT_B)
        y = lax.rem(iy + aside, 4)
        group = jnp.where(j < 16, far, near)
        r = group * 4 + y
        return {"occb": b, "rows": r}, (group * 4 + b) * 4 + y, b * 8 + r

    barrier = pltpu.get_barrier_semaphore()

    def greet(j, carry):
        pl.semaphore_signal(barrier, inc=1, device_id=partner(j)[0], device_id_type=MESH)
        return carry

    lax.fori_loop(0, PLANE - 1, greet, 0)
    for step in (1, -1, 2, -2, 4):
        pl.semaphore_signal(barrier, inc=1, device_id=a_dev(step), device_id_type=MESH)

    load_density = pltpu.make_async_copy(density_in, density, l_sem.at[0])
    load_ops = pltpu.make_async_copy(ops_in, ops, l_sem.at[1])
    load_rates = pltpu.make_async_copy(rates_in, rates, l_sem.at[2])
    load_coupling = pltpu.make_async_copy(coupling_in, coupling, l_sem.at[3])
    load_density.start()
    load_rates.start()
    load_coupling.start()
    load_ops.start()
    load_density.wait()
    kept = mask[0, 0].astype(F32)
    for part in range(2):
        dens[part * ROWS:(part + 1) * ROWS, :] = kept * density[:, part, :]
    sent_r[0] = dens[...].T
    keeps[ib] = jnp.full((8, 128), kept, F32)
    load_rates.wait()
    load_coupling.wait()
    down_a = root(ia)
    up_a = jnp.where(ia < COUNT_A - 1, root(ia + 1), 0.0)
    damp = ia.astype(F32) * rates[0] + ib.astype(F32) * rates[1]

    def factors(b):
        down_b = root(b)
        up_b = jnp.where(b < COUNT_B - 1, root(b + 1), 0.0)
        return [
            (0.0, -1.0),
            (0.0, -up_a),
            (down_a * coupling[0, 1], -down_a * coupling[0, 0]),
            (0.0, -up_b),
            (down_b * coupling[1, 1], -down_b * coupling[1, 0]),
        ]

    sibling = {"occa": ix * 2 + 1 - core}

    def remote(src, dst, send, recv, dev):
        return pltpu.make_async_remote_copy(
            src_ref=src, dst_ref=dst, send_sem=send, recv_sem=recv, device_id=dev, device_id_type=MESH
        )

    def block(index):
        return pl.ds(pl.multiple_of(index * COLS, COLS), COLS)

    def target(slot, j):
        return half_partner(j) if slot in (1, 2) else partner(j)

    def to_columns(slot, j):
        dev, col, row = target(slot, j)
        return remote(sent_r.at[slot, block(col)], cols_buf.at[slot, block(me_row)],
                      a_send.at[slot, j], a_recv.at[slot, me_row], dev)

    def to_rows(slot, j):
        dev, col, row = target(slot, j)
        return remote(pack.at[slot - 2, block(row)], cols_buf.at[slot, block(me_col)],
                      a_send.at[slot, j], a_recv.at[slot, me_col], dev)

    def start_columns(slot, first=0, last=PLANE - 1):
        def body(j, carry):
            to_columns(slot, j).start()
            return carry
        lax.fori_loop(first, last, body, 0)
        if last == PLANE - 1:
            cols_buf[slot, block(me_row), :] = sent_r[slot, block(me_col), :]

    def start_rows(slot, first=0, last=PLANE - 1):
        def body(j, carry):
            to_rows(slot, j).start()
            return carry
        lax.fori_loop(first, last, body, 0)
        if last == PLANE - 1:
            cols_buf[slot, block(me_col), :] = pack[slot - 2, block(me_row), :]

    def finish_recv(slot, by_row):
        def body(j, carry):
            dev, col, row = target(slot, j)
            index = row if by_row else col
            piece = cols_buf.at[slot, block(index)]
            remote(piece, piece, a_send.at[slot, j], a_recv.at[slot, index], dev).wait_recv()
            return carry
        lax.fori_loop(0, PLANE - 1, body, 0)

    def finish_send(slot):
        def body(j, carry):
            (to_columns if slot < 2 else to_rows)(slot, j).wait_send()
            return carry
        lax.fori_loop(0, PLANE - 1, body, 0)

    lanes = lax.broadcasted_iota(jnp.int32, (COLS, 128), 1) < 64

    def unpack(slot):
        parts = []
        for b in range(COUNT_B):
            real, imag = [], []
            for t in range(4):
                q = (b * 8 + 2 * t) * COLS
                even = cols_buf[slot, q:q + COLS, :]
                odd = cols_buf[slot, q + COLS:q + 2 * COLS, :]
                real.append(jnp.where(lanes, even, pltpu.roll(odd, 64, 1)))
                imag.append(jnp.where(lanes, pltpu.roll(even, 64, 1), odd))
            parts.append(jnp.concatenate(real, axis=1))
            parts.append(jnp.concatenate(imag, axis=1))
        return jnp.concatenate(parts, axis=0)

    def repack(slot, value, group=0):
        for b in range(COUNT_B):
            for t in range(value.shape[1] // 128):
                real = value[32 * b:32 * b + COLS, 128 * t:128 * t + 128]
                imag = value[32 * b + COLS:32 * b + 32, 128 * t:128 * t + 128]
                q = b * 8 + group * 4 + 2 * t
                pack[slot - 2, block(q), :] = jnp.where(lanes, real, pltpu.roll(imag, 64, 1))
                pack[slot - 2, block(q + 1), :] = jnp.where(lanes, pltpu.roll(real, 64, 1), imag)

    def put(side, k, row, value):
        high, low = split(value)
        count = value.shape[0]
        ghl[side, row:row + count, k * SITES:(k + 1) * SITES] = high
        ghl[side, 128 + row:128 + row + count, k * SITES:(k + 1) * SITES] = low

    def multiply(side, cols=slice(None)):
        both = jnp.dot(ghl[side], whi[:, cols], preferred_element_type=F32)
        rest = jnp.dot(ghl[side, 0:128, :], wlo[:, cols], preferred_element_type=F32)
        return both[0:128] + both[128:256] + rest

    def right(center, base):
        fields = [center, near_r.at[base], near_r.at[base + 1], near_r.at[base + 2], near_r.at[base + 3]]
        own_factors = factors(ib)
        for k, field in enumerate(fields):
            re, im = field[0:ROWS, :], field[ROWS:128, :]
            f_re, f_im = own_factors[k]
            put(0, k, 0, f_re * re + f_im * im)
            put(0, k, ROWS, f_re * im - f_im * re)

    def left(center, base):
        for b in range(COUNT_B):
            b_factors = factors(b)
            for k in range(OPS):
                source, at = center, b
                if k == 1:
                    source = near_c.at[base]
                elif k == 2:
                    source = near_c.at[base + 1]
                elif k == 3:
                    at = min(b + 1, COUNT_B - 1)
                elif k == 4:
                    at = max(b - 1, 0)
                re = source[32 * at:32 * at + COLS, :]
                im = source[32 * at + COLS:32 * at + 32, :]
                f_re, f_im = b_factors[k]
                put(1, k, 32 * b, f_re * re - f_im * im)
                put(1, k, 32 * b + COLS, f_re * im + f_im * re)

    def near_copy(kind, index, src, dst, dev):
        return remote(src, dst, n_send.at[kind, index], n_recv.at[kind, index], dev)

    def row_moves(kind, src):
        base = 4 * kind
        return [
            near_copy(kind, 0, src, near_r.at[base], a_dev(-1)),
            near_copy(kind, 1, src, near_r.at[base + 1], a_dev(1)),
            near_copy(kind, 2, src, near_r.at[base + 2], z_dev(-1)),
            near_copy(kind, 3, src, near_r.at[base + 3], z_dev(1)),
        ]

    def col_moves(kind, src):
        base = 2 * kind
        return [
            near_copy(2 + kind, 0, src, near_c.at[base], a_dev(-1)),
            near_copy(2 + kind, 1, src, near_c.at[base + 1], a_dev(1)),
        ]

    def eight(index):
        return pl.ds(pl.multiple_of(index * 8, 8), 8)

    def thirty_two(index):
        return pl.ds(pl.multiple_of(index * 32, 32), 32)

    def wide(index):
        return pl.ds(pl.multiple_of(index * 256, 256), 256)

    def sixteen(index):
        return pl.ds(pl.multiple_of(index * 16, 16), 16)

    parity = lax.rem(ix, 2)
    shares = [eight(core * 4 + parity * 2 + n) for n in range(2)]
    others = [eight(core * 4 + (1 - parity) * 2 + n) for n in range(2)]
    half_z = [remote(ops.at[:, shares[n], wide(half)], oth.at[iy, :, shares[n], :],
                     o_send.at[n], o_recv.at[n], z_dev(4)) for n in range(2)]
    half_y = [[remote(oth.at[iy, :, shares[n], :], oth.at[iy, :, shares[n], :],
                      o_send.at[1 + 3 * n + s], o_recv.at[1 + 3 * n + s], y_dev(s)) for s in (2, 1, 3)]
              for n in range(2)]
    half_x = [remote(oth.at[:, :, shares[n], :], oth.at[:, :, shares[n], :],
                     o_send.at[8 + n], o_recv.at[8 + n], a_dev((-2, 2)[n])) for n in range(2)]
    half_c = [remote(oth.at[:, :, rows, :], oth.at[:, :, rows, :],
                     o_send.at[10 + n], o_recv.at[10 + n], sibling) for n, rows in enumerate(shares + others)]

    groups = (far, near)

    def own_y(part, n):
        return remote(ops.at[:, thirty_two(core), wide(groups[part])],
                      own.at[iy, :, thirty_two(core), wide(groups[part])],
                      o_send.at[14 + 2 * part + n], o_recv.at[14 + 2 * part + n], y_dev((1, 3)[n]))

    def held(part, n, rows):
        return own.at[lax.rem(iy + (3, 1, 2)[n], 4), :, rows, wide(groups[part])]

    def passed_y(part, n):
        piece = held(part, n, sixteen(2 * core + n))
        return remote(piece, piece, o_send.at[18 + 2 * part + n], o_recv.at[18 + 2 * part + n], y_dev((1, 3)[n]))

    def own_c(part, n):
        piece = held(part, n, thirty_two(core))
        return remote(piece, piece, o_send.at[22 + 3 * part + n], o_recv.at[22 + 3 * part + n], sibling)

    own_moves = [[own_y(part, n) for n in range(2)] for part in range(2)]
    passed = [[passed_y(part, n) for n in range(2)] for part in range(2)]
    own_pairs = [[own_c(part, n) for n in range(3)] for part in range(2)]

    keep_moves = [remote(keeps.at[ib], keeps.at[ib], k_send.at[s], k_recv.at[s],
                         {"occb": lax.rem(ib + s, COUNT_B)}) for s in (1, 2, 3)]

    load_ops.wait()
    pl.semaphore_wait(barrier, PLANE - 1 + 5)
    for copy in half_z:
        copy.start()
    start_columns(0)
    for copy in own_moves[0]:
        copy.start()
    start_moves = row_moves(0, dens)
    for copy in keep_moves + start_moves:
        copy.start()

    def put_operator(part, y, rows):
        cols = wide(groups[part])
        for k in range(OPS):
            at = pl.ds(pl.multiple_of(k * SITES + half * 256 + y * ROWS, ROWS), ROWS)
            high, low = split(rows[k, :, cols])
            whi[at, cols] = high
            wlo[at, cols] = low

    def pass_on(part):
        for n in range(2):
            own_moves[part][n].wait_recv()
            passed[part][n].start()
            own_pairs[part][n].start()

    def put_own(part):
        for n in range(2):
            own_pairs[part][n].wait_recv()
            y = lax.rem(iy + (3, 1)[n], 4)
            put_operator(part, y, own.at[y])
        for copy in passed[part]:
            copy.wait_recv()
        own_pairs[part][2].start()
        own_pairs[part][2].wait_recv()
        y = lax.rem(iy + 2, 4)
        put_operator(part, y, own.at[y])

    half_z[0].wait_recv()
    for copy in half_y[0]:
        copy.start()
    put_operator(0, iy, ops)
    half_z[1].wait_recv()
    for copy in half_y[1]:
        copy.start()
    pass_on(0)
    for copy in own_moves[1]:
        copy.start()

    finish_recv(0, True)
    held_c[...] = unpack(0)
    start_cols = col_moves(0, held_c)
    for copy in start_cols:
        copy.start()
    for n in range(2):
        for copy in half_y[n]:
            copy.wait_recv()
        half_x[n].start()
        half_c[n].start()

    put_own(0)
    put_operator(1, iy, ops)
    pass_on(1)
    for copy in start_moves:
        copy.wait_recv()
    right(dens, 0)
    for n in range(2):
        half_x[n].wait_recv()
        half_c[2 + n].start()
    for copy in half_c:
        copy.wait_recv()
    for k in range(OPS):
        for y in range(4):
            at = pl.ds(pl.multiple_of(k * SITES + far * 256 + y * ROWS, ROWS), ROWS)
            high, low = split(oth[y, k])
            whi[at, wide(far)] = high
            wlo[at, wide(far)] = low

    def first_right(part):
        cols = wide(groups[part])
        value = kept * (multiply(0, cols) - damp * dens[:, cols])
        first_r[:, cols] = value
        sent_r[1, cols, :] = value.T
        start_columns(1, 16 * part, 16 + 15 * part)

    def first_left(part):
        cols = wide(groups[part])
        value = kept_c * multiply(1, cols)
        first_c[:, cols] = value
        repack(2, value, groups[part])
        start_rows(2, 16 * part, 16 + 15 * part)

    first_right(0)
    for copy in start_cols:
        copy.wait_recv()
    for copy in keep_moves:
        copy.wait_recv()
    kept_c = jnp.concatenate(
        [jnp.broadcast_to(keeps[b, 0:1, 0:1], (2 * COLS, SITES // 2)) for b in range(COUNT_B)], axis=0
    )
    left(held_c, 0)
    first_left(0)

    put_own(1)
    for k in range(OPS):
        source = pl.ds(pl.multiple_of(k * SITES + near * 256, 256), 256)
        target_rows = pl.ds(pl.multiple_of(k * SITES + far * 256, 256), 256)
        whi[target_rows, wide(near)] = whi[source, wide(far)].T
        wlo[target_rows, wide(near)] = wlo[source, wide(far)].T
    first_right(1)
    first_left(1)

    finish_recv(1, True)
    first_c[...] += unpack(1)
    next_cols = col_moves(1, first_c)
    for copy in next_cols:
        copy.start()
    finish_recv(2, False)
    first_r[...] += cols_buf[2].T
    next_moves = row_moves(1, first_r)
    for copy in next_moves:
        copy.start()

    for copy in next_cols:
        copy.wait_recv()
    left(first_c, 2)
    repack(3, multiply(1))
    start_rows(3)

    for copy in next_moves:
        copy.wait_recv()
    right(first_r, 4)
    second = multiply(0) - damp * first_r[...]
    finish_recv(3, False)
    second = kept * (second + cols_buf[3].T)
    result = dens[...] + TIME_STEP * first_r[...] + (0.5 * TIME_STEP * TIME_STEP) * second
    for part in range(2):
        out[:, part, :] = result[part * ROWS:(part + 1) * ROWS]

    for copy in half_z + half_y[0] + half_y[1] + half_x + half_c:
        copy.wait_send()
    for slot in range(4):
        finish_send(slot)
    for part in range(2):
        for copy in own_moves[part] + passed[part] + own_pairs[part]:
            copy.wait_send()
    for copy in keep_moves + start_moves + start_cols + next_cols + next_moves:
        copy.wait_send()


def shards(density, operators, rates, coupling, keep_mask):
    vmem = pl.BlockSpec(memory_space=pltpu.VMEM)
    smem = pl.BlockSpec(memory_space=pltpu.SMEM)
    hbm = pl.BlockSpec(memory_space=pl.ANY)
    dma = pltpu.SemaphoreType.DMA
    result = pl.pallas_call(
        kernel,
        out_shape=jax.ShapeDtypeStruct((ROWS, 2, SITES), F32),
        in_specs=[hbm, hbm, smem, hbm, hbm],
        out_specs=vmem,
        scratch_shapes=[
            pltpu.SMEM((2,), F32),
            pltpu.SMEM((2, 2), F32),
            pltpu.VMEM((ROWS, 2, SITES), F32),
            pltpu.VMEM((OPS, ROWS, SITES), F32),
            pltpu.VMEM((2 * ROWS, SITES), F32),
            pltpu.VMEM((4, OPS, ROWS, SITES), F32),
            pltpu.VMEM((4, OPS, ROWS, SITES // 2), F32),
            pltpu.VMEM((OPS * SITES, SITES), BF16),
            pltpu.VMEM((OPS * SITES, SITES), BF16),
            pltpu.VMEM((2, 256, OPS * SITES), BF16),
            pltpu.VMEM((2, SITES, 128), F32),
            pltpu.VMEM((4, SITES, 128), F32),
            pltpu.VMEM((128, SITES), F32),
            pltpu.VMEM((2, SITES, 128), F32),
            pltpu.VMEM((128, SITES), F32),
            pltpu.VMEM((128, SITES), F32),
            pltpu.VMEM((8, 128, SITES), F32),
            pltpu.VMEM((4, 128, SITES), F32),
            pltpu.VMEM((COUNT_B, 8, 128), F32),
            dma((4, PLANE)),
            dma((4, PLANE)),
            dma((4, 4)),
            dma((4, 4)),
            dma((4,)),
            dma((4,)),
            dma((28,)),
            dma((28,)),
            dma((4,)),
        ],
        compiler_params=pltpu.CompilerParams(
            collective_id=0, has_side_effects=True, vmem_limit_bytes=60 << 20
        ),
    )(rates, coupling, keep_mask, density.reshape(ROWS, 2, SITES), operators)
    return result.reshape(density.shape)


def solution(mesh):
    placed = (
        P("rows", "occa", "occb", None, None),
        P(None, "rows", None),
        P(),
        P(),
        P("occa", "occb"),
    )
    return jax.shard_map(
        shards,
        mesh=mesh,
        in_specs=placed,
        out_specs=P("rows", "occa", "occb", None, None),
        check_vma=False,
    )
```
